512 devices in a mesh: section: 8 (over z_lo), dp: 64 (over z_hi, x, y, core).
Axes of the slice: x: 4, y: 4, z: 16 (z_hi: 2, z_lo: 8; z = z_hi * 8 + z_lo), core: 2. Of those that a mesh axis runs over, the one named last changes fastest.
Arguments:
- patches: bfloat16 [8, 8192, 2048], P('section', 'dp'), may hold values from -6 to 6
- pack_dest: int32 [8, 8192], P('section', 'dp'), may hold values from 0 to 8191, as said below
- seg_ids: int32 [8, 8192], P('section', 'dp'), may hold values from 0 to 191, as said below
- w_patch_in: bfloat16 [8, 2048, 256], P('section', 'dp'), may hold values from -0.125 to 0.125
- w_patch_out: bfloat16 [8, 256, 2048], P('section', 'dp'), may hold values from -0.375 to 0.375
- w_query: bfloat16 [8, 2048, 1024], P('section', 'dp')
- w_keyval: bfloat16 [8, 2048, 512], P('section', 'dp')
- w_attn_out: bfloat16 [8, 1024, 2048], P('section', 'dp'), may hold values from -0.75 to 0.75
Outputs:
- handed: bfloat16 [8, 8192, 2048], P('section', 'dp')
The draws below stay inside these ranges and needn't reach their ends.
Inputs may be any that keep to these rules, and one draw needn't show every extreme that they name: For each micro-batch a permutation of the 8192 rows; the rows i of one aligned block of 128 rows send at most 4 rows into any one aligned block of pack_dest values, and some pair of blocks reaches 4. `seg_ids`: never falling along a micro-batch's rows, starting at 0 and rising by one where a document starts; a document starts at row 0, at every row r with r % 64 == 32, and in exactly 63 of the spans between two such rows at one other row, never at a multiple of 64; each document has 1 to 64 rows and one has exactly 64.
All inputs are finite; a program needn't handle non-finite values.
Results may differ from the reference program's by a relative error of at most 0.015.
The reference program's roundings to bfloat16 on the way count: a program that leaves them out, or rounds other values in their place, can miss the bound.
Values may be sent and summed in bfloat16 or wider, within the bound.
A program may use at most 64 MiB of HBM per device.

```python
import math
import jax
import jax.numpy as jnp
from jax import lax

D = 2048
HEADS = 16
KV_HEADS = 4
HEAD_WIDTH = 64
EMB_HID = 256
TOK_DEV = 128
DOC_MAX = 64
MB = 8
TOKENS = 8192
RAW = 2048
QW = 1024


def query_table(key):
    return jax.random.normal(jax.random.fold_in(key, 101), (MB, D, HEADS * HEAD_WIDTH), jnp.float32) * D ** (-0.5)


def draw_w_query(key, part):
    return query_table(key).astype(jnp.bfloat16)


def draw_w_keyval(key, part):
    kv_width = KV_HEADS * HEAD_WIDTH
    key_part = jax.random.normal(jax.random.fold_in(key, 102), (MB, D, kv_width), jnp.float32) * D ** (-0.5)
    value_part = jax.random.normal(jax.random.fold_in(key, 103), (MB, D, kv_width), jnp.float32) * D ** (-0.5)
    return jnp.concatenate([key_part, value_part], axis=2).astype(jnp.bfloat16)


def packing_map(key):
    devices = TOKENS // TOK_DEV
    base = TOK_DEV // devices
    key_amount, key_order, key_dest, key_source = jax.random.split(key, 4)
    amounts = jax.random.randint(key_amount, (devices // 2,), 0, base + 1).astype(jnp.int32).at[0].set(base)
    pattern = jax.random.permutation(key_order, jnp.concatenate([amounts, -amounts]))
    sources = jnp.arange(devices, dtype=jnp.int32)
    counts = base + pattern[(sources[None, :] - sources[:, None]) % devices]
    ends = jnp.cumsum(counts, axis=1)
    before = jnp.cumsum(counts, axis=0) - counts
    positions = jnp.arange(TOK_DEV, dtype=jnp.int32)
    dest_device = jnp.sum((positions[None, :, None] >= ends[:, None, :]).astype(jnp.int32), axis=2)
    starts = jnp.take_along_axis(ends - counts, dest_device, axis=1)
    arrival = jnp.take_along_axis(before, dest_device, axis=1) + positions[None, :] - starts

    def shuffled(subkey):
        return jax.random.permutation(subkey, TOK_DEV).astype(jnp.int32)
    dest_order = jax.vmap(shuffled)(jax.random.split(key_dest, devices))
    source_order = jax.vmap(shuffled)(jax.random.split(key_source, devices))
    slots = dest_order[dest_device, arrival]
    flat = dest_device * TOK_DEV + slots
    result = jnp.zeros((devices, TOK_DEV), jnp.int32).at[sources[:, None], source_order].set(flat)
    return result.reshape(TOKENS)


def draw_pack_dest(key, part):
    return jax.vmap(packing_map)(jax.random.split(key, MB)).astype(jnp.int32)


def draw_seg_ids(key, part):
    windows = TOKENS // DOC_MAX
    half = DOC_MAX // 2
    chosen = windows // 2 - 1
    key_take, key_long, key_cut = jax.random.split(jax.random.fold_in(key, 201), 3)
    longest = jax.random.randint(key_long, (MB,), 0, windows - 1).astype(jnp.int32)
    window_ids = jnp.arange(windows, dtype=jnp.int32)

    def ordering(subkey):
        return jax.random.permutation(subkey, windows).astype(jnp.int32)
    scores = jax.vmap(ordering)(jax.random.split(key_take, MB))
    barred = (window_ids[None, :] == longest[:, None]) | (window_ids[None, :] == windows - 1)
    scores = scores + windows * barred.astype(jnp.int32)
    ranks = jnp.argsort(jnp.argsort(scores, axis=1, stable=True), axis=1, stable=True).astype(jnp.int32)
    take = (ranks < chosen).astype(jnp.int32)
    cut = jax.random.randint(key_cut, (MB, windows), 1, DOC_MAX - 1).astype(jnp.int32)
    cut = cut + (cut >= half).astype(jnp.int32)
    positions = jnp.arange(TOKENS, dtype=jnp.int32)
    shifted = jnp.maximum(positions - half, 0)
    window = jnp.minimum(shifted // DOC_MAX, windows - 1)
    within = shifted % DOC_MAX
    after = (positions >= half).astype(jnp.int32)
    forced = after * (within == 0).astype(jnp.int32)
    take_here = jnp.take_along_axis(take, jnp.broadcast_to(window[None, :], (MB, TOKENS)), axis=1)
    cut_here = jnp.take_along_axis(cut, jnp.broadcast_to(window[None, :], (MB, TOKENS)), axis=1)
    extra = after[None, :] * take_here * (within[None, :] == cut_here).astype(jnp.int32)
    flags = forced[None, :] + extra
    return jnp.cumsum(flags, axis=1).astype(jnp.int32)


def levels(key, shape, cuts, smallest, top_value):
    factor_of, own = 1.0, jax.random.fold_in(key, 6)
    for dim, shards_of in cuts:
        heights = jnp.exp(jax.random.uniform(jax.random.fold_in(own, dim), (shards_of,), jnp.float32, smallest / len(cuts), top_value / len(cuts)))
        factor_of = factor_of * jnp.repeat(heights, shape[dim] // shards_of).reshape([-1 if axis == dim else 1 for axis in range(len(shape))])
    return factor_of


def normal_values(stream_key, dims, spread, most, cuts=(), held_as=jnp.bfloat16):
    values = spread * jax.random.normal(stream_key, dims, jnp.float32)
    if cuts:
        values = values * levels(stream_key, dims, cuts, -0.22, 0.18)
    return jnp.clip(values, -most, most).astype(held_as)


def setup_inputs(seed: int = 0) -> dict:
    keys = jax.random.split(jax.random.key(seed), 9)
    patches = normal_values(keys[0], (MB, TOKENS, RAW), 1.0, 6.0, ((0, 8), (1, 64)))
    pack_dest = draw_pack_dest(jax.random.fold_in(keys[8], 71), 0)
    seg_ids = draw_seg_ids(jax.random.fold_in(keys[8], 71), 0)
    w_patch_in = normal_values(keys[3], (MB, RAW, EMB_HID), RAW ** -0.5, 0.125, ((0, 8), (1, 64)))
    w_patch_out = normal_values(keys[4], (MB, EMB_HID, D), EMB_HID ** -0.5, 0.375, ((0, 8), (1, 64)))
    w_query = draw_w_query(jax.random.fold_in(keys[8], 71), 0)
    w_keyval = draw_w_keyval(jax.random.fold_in(keys[8], 71), 0)
    w_attn_out = normal_values(keys[7], (MB, QW, D), HEAD_WIDTH ** -0.5, 0.75, ((0, 8), (1, 64)))
    return {"patches": patches, "pack_dest": pack_dest, "seg_ids": seg_ids, "w_patch_in": w_patch_in, "w_patch_out": w_patch_out, "w_query": w_query, "w_keyval": w_keyval, "w_attn_out": w_attn_out}


def attend_rows(queries, keyval, query_seg, key_seg, query_pos, key_pos):
    row_count = queries.shape[0]
    key_count = keyval.shape[0]
    repeat = HEADS // KV_HEADS
    kv_width = KV_HEADS * HEAD_WIDTH
    per_head_queries = queries.reshape(row_count, KV_HEADS, repeat, HEAD_WIDTH).astype(jnp.float32)
    per_head_keys = keyval[:, :kv_width].reshape(key_count, KV_HEADS, HEAD_WIDTH).astype(jnp.float32)
    per_head_values = keyval[:, kv_width:].reshape(key_count, KV_HEADS, HEAD_WIDTH).astype(jnp.float32)
    attention_logits = jnp.einsum('jiyp,aip->iyja', per_head_queries, per_head_keys) / math.sqrt(HEAD_WIDTH)
    allowed = (query_seg[:, None] == key_seg[None, :]) & (key_pos[None, :] >= 0) & (key_pos[None, :] <= query_pos[:, None])
    attention_logits = jnp.where(allowed[None, None], attention_logits, -jnp.inf)
    row_max = lax.optimization_barrier(jnp.max(attention_logits, axis=-1, keepdims=True))
    expon = jnp.exp(attention_logits - row_max)
    attention_probabilities = (expon / lax.optimization_barrier(jnp.sum(expon, axis=-1, keepdims=True))).astype(jnp.bfloat16)
    attention_probabilities = lax.optimization_barrier(attention_probabilities).astype(jnp.float32)
    attended_values = jnp.einsum('iolf,fia->lioa', attention_probabilities, per_head_values)
    return attended_values.astype(jnp.bfloat16).reshape(row_count, HEADS * HEAD_WIDTH)

def one_batch(patches, pack_dest, seg_ids, w_patch_in, w_patch_out, w_query, w_keyval, w_attn_out):
    first_layer = jax.nn.gelu(jnp.dot(patches, w_patch_in, preferred_element_type=jnp.float32)).astype(jnp.bfloat16)
    embedded = jnp.dot(first_layer, w_patch_out, preferred_element_type=jnp.float32).astype(jnp.bfloat16)
    packed = jnp.zeros_like(embedded).at[pack_dest].set(embedded)
    residual = packed.astype(jnp.float32)
    normed = (residual * lax.rsqrt(lax.optimization_barrier(jnp.mean(residual * residual, axis=-1, keepdims=True)) + 1e-05)).astype(jnp.bfloat16)
    queries = jnp.dot(normed, w_query, preferred_element_type=jnp.float32).astype(jnp.bfloat16)
    keyval = jnp.dot(normed, w_keyval, preferred_element_type=jnp.float32).astype(jnp.bfloat16)
    padded_kv = jnp.concatenate([jnp.zeros((TOK_DEV, keyval.shape[1]), jnp.bfloat16), keyval], axis=0)
    padded_seg = jnp.concatenate([jnp.zeros((TOK_DEV,), jnp.int32), seg_ids.astype(jnp.int32)], axis=0)

    def block_rows(block_index):
        offset = (block_index * TOK_DEV).astype(jnp.int32)
        query_block = lax.dynamic_slice_in_dim(queries, offset, TOK_DEV, 0)
        key_block = lax.dynamic_slice_in_dim(padded_kv, offset, 2 * TOK_DEV, 0)
        query_seg = lax.dynamic_slice_in_dim(seg_ids.astype(jnp.int32), offset, TOK_DEV, 0)
        key_seg = lax.dynamic_slice_in_dim(padded_seg, offset, 2 * TOK_DEV, 0)
        query_pos = offset + jnp.arange(TOK_DEV, dtype=jnp.int32)
        key_pos = offset - TOK_DEV + jnp.arange(2 * TOK_DEV, dtype=jnp.int32)
        return attend_rows(query_block, key_block, query_seg, key_seg, query_pos, key_pos)
    attended_values = lax.map(block_rows, jnp.arange(TOKENS // TOK_DEV, dtype=jnp.int32)).reshape(TOKENS, HEADS * HEAD_WIDTH)
    projected = jnp.dot(attended_values, w_attn_out, preferred_element_type=jnp.float32)
    return (projected + residual).astype(jnp.bfloat16)

def reference(patches, pack_dest, seg_ids, w_patch_in, w_patch_out, w_query, w_keyval, w_attn_out):

    def per_batch(operands):
        return one_batch(*operands)
    outputs = lax.map(per_batch, (patches, pack_dest, seg_ids, w_patch_in, w_patch_out, w_query, w_keyval, w_attn_out))
    return jnp.roll(outputs, 1, axis=0)
```

```python
import math

import jax
import jax.numpy as jnp
from jax import lax
from jax.experimental import pallas as pl
from jax.experimental.pallas import tpu as pltpu
from jax.sharding import PartitionSpec as P

HEADS = 16
KV_HEADS = 4
HEAD_WIDTH = 64
ROWS = 128
TAIL = 32
SLOTS = 4
PEERS = 64
MESH = pl.DeviceIdType.MESH
F32 = jnp.float32
BF16 = jnp.bfloat16
ALL = slice(None)


def iota(shape, dim):
    return lax.broadcasted_iota(jnp.int32, shape, dim)


def dot(a, b):
    return jnp.dot(a, b, preferred_element_type=F32)


def dot_nt(a, b):
    return lax.dot_general(a, b, (((1,), (1,)), ((), ())), preferred_element_type=F32)


def kernel(
    patches,
    dest,
    seg,
    w_in,
    w_out,
    w_query,
    w_keyval,
    w_proj,
    out,
    rows_v,
    g_in,
    g_out,
    g_qkv,
    g_proj,
    out_piece,
    sent,
    got,
    sent_at,
    got_at,
    segs,
    packed,
    tail,
    emb,
    normed,
    qkv,
    ctx,
    ss,
    rs,
    a2a_ss,
    a2a_rs,
    local,
):
    s = lax.axis_index("section")
    d = lax.axis_index("dp")
    h, x, y, c = d // 32, (d // 8) % 4, (d // 2) % 4, d % 2
    s_next, s_prev = (s + 1) % 8, (s + 7) % 8
    d_next, d_prev = (d + 1) % PEERS, (d + PEERS - 1) % PEERS
    x_by = {1: (x + 1) % 4, -1: (x + 3) % 4, 2: (x + 2) % 4}
    y_by = {1: (y + 1) % 4, -1: (y + 3) % 4, 2: (y + 2) % 4}
    z = h * 8 + s
    z_next, z_prev = (z + 1) % 16, (z + 15) % 16
    near, far = z_prev // 8, 1 - z_prev // 8

    def at(hh, xx, yy, cc):
        return hh * 32 + xx * 8 + yy * 2 + cc

    def x_peer(by):
        return (s, at(h, x_by[by], y, c))

    def y_peer(by):
        return (s, at(h, x, y_by[by], c))

    ahead = (s_next, at(z_next // 8, x, y, c))
    partner = (s, at(1 - h, x, y, c))
    sibling = (s, at(h, x, y, 1 - c))

    load_rows = pltpu.make_async_copy(patches, rows_v, local.at[0])
    load_rows.start()
    load_in = pltpu.make_async_copy(w_in, g_in.at[h, x, y, c], local.at[1])
    load_in.start()

    barrier = pltpu.get_barrier_semaphore()

    def greet(k, carry):
        pl.semaphore_signal(barrier, inc=1, device_id=(s_prev, k), device_id_type=MESH)
        return carry

    lax.fori_loop(0, PEERS, greet, 0)
    for peer in (
        partner,
        sibling,
        x_peer(1),
        x_peer(-1),
        y_peer(1),
        y_peer(-1),
        (s, d_prev),
    ):
        pl.semaphore_signal(barrier, inc=1, device_id=peer, device_id_type=MESH)

    wide = w_out[...].astype(F32)
    out_piece[...] = jnp.concatenate(
        [wide[:, 512 * j : 512 * (j + 1)] for j in range(4)], axis=0
    ).astype(BF16)

    to = dest[...]
    to_dev, to_slot = to // ROWS, to % ROWS
    match = (iota((PEERS, ROWS), 0) == to_dev).astype(F32)
    before = (iota((ROWS, ROWS), 0) < iota((ROWS, ROWS), 1)).astype(F32)
    earlier = dot(match.astype(BF16), before.astype(BF16))
    rank = jnp.sum(earlier * match, axis=0, keepdims=True).astype(jnp.int32)
    places = dot_nt(
        (match * (to_slot + 1).astype(F32)).astype(BF16),
        (iota((ROWS, ROWS), 0) % SLOTS == rank).astype(BF16),
    )
    sent_at[...] = (places.astype(jnp.int32) - 1).reshape(PEERS, 1, ROWS)
    line = iota((8 * PEERS, ROWS), 0)
    chosen = (line // 8 == to_dev) & (line % SLOTS == rank)
    pick_low = (chosen & (line % 8 < SLOTS)).astype(F32).astype(BF16)
    pick_high = (chosen & (line % 8 >= SLOTS)).astype(F32).astype(BF16)

    load_in.wait()
    pl.semaphore_wait(barrier, PEERS + 7)

    copies = []

    def send(src, dst, peer):
        i = len(copies)
        copy = pltpu.make_async_remote_copy(
            src_ref=src,
            dst_ref=dst,
            send_sem=ss.at[i],
            recv_sem=rs.at[i],
            device_id=peer,
            device_id_type=MESH,
        )
        copy.start()
        copies.append(copy)
        return copy

    def spread(ref, peer):
        return send(ref, ref, peer)

    in_far = spread(g_in.at[h, x, y, c], partner)
    out_near = send(out_piece, g_out.at[h, x, y, c], ahead)
    q_near = send(w_query, g_qkv.at[h, x, y, c, :, pl.ds(0, 1024)], ahead)
    kv_near = send(w_keyval, g_qkv.at[h, x, y, c, :, pl.ds(1024, 512)], ahead)
    o_near = send(w_proj, g_proj.at[h, x, y, c], ahead)
    seg_own = send(seg, segs.at[0], (s_next, d))
    seg_tail = send(seg, segs.at[1], (s_next, d_next))

    class Unit:
        def __init__(self, ref, hh):
            self.ref, self.hh = ref, hh
            self.width = ref.shape[-1]
            self.split = self.width >= 512
            self.core = []

        def block(self, lane, first, second, part=None):
            half = self.width // 2
            low, count = lane * half, half
            if part is not None and self.split:
                low, count = low + part * (half // 2), half // 2
            xx, yy = (first, second) if lane == 0 else (second, first)
            return self.ref.at[self.hh, xx, yy, c, :, pl.ds(low, count)]

        def one(self):
            self.c1 = {}
            for lane in (0, 1):
                a, b = (x, y) if lane == 0 else (y, x)
                peer = x_peer if lane == 0 else y_peer
                for way in (1, -1):
                    self.c1[lane, way] = spread(self.block(lane, a, b), peer(way))

        def forward(self, lane, way):
            return self.split or (way == 1) == (lane == 0)

        def two(self):
            self.c2 = {}
            for way in (1, -1):
                for lane in (0, 1):
                    by, b = (x_by, y) if lane == 0 else (y_by, x)
                    peer = x_peer if lane == 0 else y_peer
                    self.c1[lane, way].wait_recv()
                    if self.forward(lane, way):
                        self.c2[lane, way] = spread(
                            self.block(lane, by[-way], b, (1 - way) // 2), peer(way)
                        )

        def three(self):
            self.c3 = {}
            for lane in (0, 1):
                b = y if lane == 0 else x
                peer = y_peer if lane == 0 else x_peer
                for way in (1, -1):
                    if (lane, way) in self.c2:
                        self.c2[lane, way].wait_recv()
                whole = self.block(lane, ALL, b)
                for way in (1, -1):
                    self.c3[lane, way] = spread(whole, peer(way))
                self.core.append(spread(whole, sibling))

        def four(self):
            self.c4 = {}
            for way in (1, -1):
                for lane in (0, 1):
                    by = y_by if lane == 0 else x_by
                    peer = y_peer if lane == 0 else x_peer
                    self.c3[lane, way].wait_recv()
                    if self.forward(lane, way):
                        self.c4[lane, way] = spread(
                            self.block(lane, ALL, by[-way], (1 - way) // 2), peer(way)
                        )
                    self.core.append(spread(self.block(lane, ALL, by[-way]), sibling))

        def five(self):
            for lane in (0, 1):
                by = y_by if lane == 0 else x_by
                for way in (1, -1):
                    if (lane, way) in self.c4:
                        self.c4[lane, way].wait_recv()
                self.core.append(spread(self.block(lane, ALL, by[2]), sibling))

        def six(self):
            for copy in self.core:
                copy.wait_recv()

    u_in, u_out = Unit(g_in, ALL), Unit(g_out, ALL)
    u_qkv_n, u_qkv_f = Unit(g_qkv, near), Unit(g_qkv, far)
    u_o_n, u_o_f = Unit(g_proj, near), Unit(g_proj, far)

    def relay(ref, *arrived):
        for copy in arrived:
            copy.wait_recv()
        return spread(ref.at[near, x, y, c], partner)

    out_far = relay(g_out, out_near)
    qkv_far = relay(g_qkv, q_near, kv_near)
    in_far.wait_recv()
    u_in.one()
    u_qkv_n.one()
    o_far = relay(g_proj, o_near)

    u_in.two()
    u_qkv_n.two()
    u_in.three()
    u_qkv_n.three()
    u_in.four()
    out_far.wait_recv()
    u_out.one()
    u_o_n.one()
    u_in.five()
    u_qkv_n.four()
    u_out.two()
    u_o_n.two()

    load_rows.wait()
    u_in.six()
    first = jax.nn.gelu(dot(rows_v[...], g_in[...].reshape(2048, 256))).astype(BF16)
    picked = dot(pick_low, first[:, :128]) + dot(pick_high, first[:, 128:])
    sent[...] = picked.reshape(PEERS, 8, 128).astype(BF16)

    def exchange(k, carry):
        e = (d + k) % PEERS
        for src, dst, i in ((sent, got, 0), (sent_at, got_at, 1)):
            pltpu.make_async_remote_copy(
                src_ref=src.at[e],
                dst_ref=dst.at[d],
                send_sem=a2a_ss.at[i],
                recv_sem=a2a_rs.at[i],
                device_id=(s_next, e),
                device_id_type=MESH,
            ).start()
        return carry

    lax.fori_loop(0, PEERS, exchange, 0)

    u_out.three()
    u_o_n.three()
    qkv_far.wait_recv()
    u_qkv_f.one()
    u_qkv_n.five()
    u_out.four()
    u_o_n.four()
    u_qkv_f.two()
    o_far.wait_recv()
    u_o_f.one()
    u_out.five()
    u_o_n.five()
    u_qkv_f.three()
    u_o_f.two()

    pltpu.make_async_copy(got, got, a2a_rs.at[0]).wait()
    pltpu.make_async_copy(got_at, got_at, a2a_rs.at[1]).wait()
    place = got_at[...]
    source = iota((PEERS, 1, ROWS), 0)
    lane = iota((PEERS, 1, ROWS), 2)
    valued = [
        jnp.sum(jnp.where(source == (lane + ROWS * q) // 8, place, 0), axis=0)
        for q in range(4)
    ]
    valued = jnp.concatenate(valued, axis=1)
    column = iota((ROWS, 8 * PEERS), 1)
    put = iota((ROWS, 8 * PEERS), 0) == valued
    arrived = got[...].astype(F32).reshape(8 * PEERS, 128).astype(BF16)
    put_low = (put & (column % 8 < SLOTS)).astype(F32).astype(BF16)
    put_high = (put & (column % 8 >= SLOTS)).astype(F32).astype(BF16)
    packed[:, :128] = dot(put_low, arrived).astype(BF16)
    packed[:, 128:] = dot(put_high, arrived).astype(BF16)
    tail_copy = send(packed.at[pl.ds(ROWS - TAIL, TAIL)], tail, (s, d_next))

    u_qkv_f.four()
    u_o_f.three()

    tail_copy.wait_recv()
    u_out.six()
    both = jnp.concatenate([packed[...], tail[...]], axis=0)
    spreader = (
        iota((256, 1024), 0) == 4 * (iota((256, 1024), 1) // 16) + iota((256, 1024), 1) % 4
    )
    wide = dot(both, spreader.astype(F32).astype(BF16))
    group = (iota((ROWS + TAIL, 1024), 1) % 16) // 4
    for j in range(4):
        lhs = jnp.where(group == j, wide, 0.0).astype(BF16)
        emb[:, pl.ds(512 * j, 512)] = dot(lhs, g_out[...].reshape(1024, 512)).astype(BF16)
    residual = emb[...].astype(F32)
    scale = lax.rsqrt(jnp.mean(residual * residual, axis=-1, keepdims=True) + 1e-05)
    normed[...] = (residual * scale).astype(BF16)

    u_qkv_f.five()
    u_o_f.four()
    u_qkv_n.six()
    u_qkv_f.six()

    def project(j, carry):
        cols = pl.ds(pl.multiple_of(j * 256, 256), 256)
        weights = g_qkv[:, :, :, :, :, cols].reshape(2048, 256)
        qkv[:, cols] = dot(normed[...], weights).astype(BF16)
        return carry

    lax.fori_loop(0, 6, project, 0)

    seg_own.wait_recv()
    seg_tail.wait_recv()
    own = segs[0]
    square = iota((ROWS, ROWS), 0) == iota((ROWS, ROWS), 1)
    row_seg = jnp.sum(jnp.where(square, own, 0), axis=1, keepdims=True)
    key_seg = jnp.concatenate([own, pltpu.roll(segs[1], TAIL, 1)], axis=1)[:, : ROWS + TAIL]
    key = iota((ROWS, ROWS + TAIL), 1)
    row = iota((ROWS, ROWS + TAIL), 0)
    allowed = (key_seg == row_seg) & ((key <= row) | ((key >= ROWS) & (d > 0)))
    low = iota((ROWS + TAIL, 128), 1) < HEAD_WIDTH
    zero = jnp.zeros((ROWS + TAIL, 128), F32)

    def sides(tile, group):
        tile = tile.astype(F32)
        turned = pltpu.roll(tile, HEAD_WIDTH, 1)
        here, there = (tile, turned) if group == 0 else (turned, tile)
        return (
            jnp.where(low, here, zero).astype(BF16),
            jnp.where(low, zero, there).astype(BF16),
        )

    for pair in range(2):
        keys_tile = qkv[:, pl.ds(1024 + 128 * pair, 128)]
        values_tile = qkv[:, pl.ds(1280 + 128 * pair, 128)]
        for group in range(2):
            keys = sides(keys_tile, group)
            values = sides(values_tile, group)
            for tile in range(2):
                cols = 256 * (2 * pair + group) + 128 * tile
                queries = qkv[:ROWS, pl.ds(cols, 128)]
                total = None
                for side in range(2):
                    scores = dot_nt(queries, keys[side]) * (1.0 / math.sqrt(HEAD_WIDTH))
                    scores = jnp.where(allowed, scores, -jnp.inf)
                    expon = jnp.exp(scores - jnp.max(scores, axis=-1, keepdims=True))
                    probs = (expon / jnp.sum(expon, axis=-1, keepdims=True)).astype(BF16)
                    part = dot(probs, values[side])
                    total = part if total is None else total + part
                ctx[:, pl.ds(cols, 128)] = total.astype(BF16)

    u_o_f.five()
    u_o_n.six()
    u_o_f.six()

    def finish(j, carry):
        cols = pl.ds(pl.multiple_of(j * 256, 256), 256)
        weights = g_proj[:, :, :, :, :, cols].reshape(1024, 256)
        added = dot(ctx[...], weights) + emb[pl.ds(0, ROWS), cols].astype(F32)
        out[:, cols] = added.astype(BF16)
        return carry

    lax.fori_loop(0, 8, finish, 0)

    for copy in copies:
        copy.wait_send()
    pltpu.make_async_copy(sent, sent, a2a_ss.at[0]).wait()
    pltpu.make_async_copy(sent_at, sent_at, a2a_ss.at[1]).wait()


def on_device(patches, pack_dest, seg_ids, w_patch_in, w_patch_out, w_query, w_keyval, w_attn_out):
    vmem = pl.BlockSpec(memory_space=pltpu.VMEM)
    hbm = pl.BlockSpec(memory_space=pl.ANY)
    grid = (2, 4, 4, 2)
    out = pl.pallas_call(
        kernel,
        out_shape=jax.ShapeDtypeStruct((ROWS, 2048), BF16),
        in_specs=[hbm, vmem, vmem, hbm, vmem, hbm, hbm, hbm],
        out_specs=vmem,
        scratch_shapes=[
            pltpu.VMEM((ROWS, 2048), BF16),
            pltpu.VMEM(grid + (32, 256), BF16),
            pltpu.VMEM(grid + (16, 512), BF16),
            pltpu.VMEM(grid + (32, 1536), BF16),
            pltpu.VMEM(grid + (16, 2048), BF16),
            pltpu.VMEM((16, 512), BF16),
            pltpu.VMEM((PEERS, 8, 128), BF16),
            pltpu.VMEM((PEERS, 8, 128), BF16),
            pltpu.VMEM((PEERS, 1, ROWS), jnp.int32),
            pltpu.VMEM((PEERS, 1, ROWS), jnp.int32),
            pltpu.VMEM((2, 1, ROWS), jnp.int32),
            pltpu.VMEM((ROWS, 256), BF16),
            pltpu.VMEM((TAIL, 256), BF16),
            pltpu.VMEM((ROWS + TAIL, 2048), BF16),
            pltpu.VMEM((ROWS + TAIL, 2048), BF16),
            pltpu.VMEM((ROWS + TAIL, 1536), BF16),
            pltpu.VMEM((ROWS, 1024), BF16),
            pltpu.SemaphoreType.DMA((180,)),
            pltpu.SemaphoreType.DMA((180,)),
            pltpu.SemaphoreType.DMA((2,)),
            pltpu.SemaphoreType.DMA((2,)),
            pltpu.SemaphoreType.DMA((2,)),
        ],
        compiler_params=pltpu.CompilerParams(
            collective_id=0, has_side_effects=True, vmem_limit_bytes=48 << 20
        ),
        name="layer",
    )(
        patches[0],
        pack_dest,
        seg_ids,
        w_patch_in[0],
        w_patch_out[0],
        w_query[0],
        w_keyval[0],
        w_attn_out[0],
    )
    return out[None]


def solution(mesh):
    in_specs = (
        P("section", "dp", None),
        P("section", "dp"),
        P("section", "dp"),
        P("section", "dp", None),
        P("section", "dp", None),
        P("section", "dp", None),
        P("section", "dp", None),
        P("section", "dp", None),
    )
    out_specs = P("section", "dp", None)
    return jax.shard_map(
        on_device, mesh=mesh, in_specs=in_specs, out_specs=out_specs, check_vma=False
    )
```

```python
import math

import jax
import jax.numpy as jnp
from jax import lax
from jax.experimental import pallas as pl
from jax.experimental.pallas import tpu as pltpu
from jax.sharding import PartitionSpec as P

HEADS = 16
KV_HEADS = 4
HEAD_WIDTH = 64
ROWS = 128
TAIL = 32
SLOTS = 4
PEERS = 64
MESH = pl.DeviceIdType.MESH
F32 = jnp.float32
BF16 = jnp.bfloat16
ALL = slice(None)


def iota(shape, dim):
    return lax.broadcasted_iota(jnp.int32, shape, dim)


def dot(a, b):
    return jnp.dot(a, b, preferred_element_type=F32)


def dot_nt(a, b):
    return lax.dot_general(a, b, (((1,), (1,)), ((), ())), preferred_element_type=F32)


def kernel(
    patches,
    dest_hbm,
    seg_hbm,
    w_in,
    w_out_hbm,
    w_query,
    w_keyval,
    w_proj,
    out,
    dest,
    seg,
    w_out,
    rows_v,
    g_in,
    g_out,
    g_qkv,
    g_proj,
    out_piece,
    held_qkv,
    held_o,
    sent,
    got,
    packed,
    tail,
    emb,
    normed,
    qkv,
    ctx,
    ss,
    rs,
    a2a_ss,
    a2a_rs,
    local,
    ready,
):
    s = lax.axis_index("section")
    d = lax.axis_index("dp")
    h, x, y, c = d // 32, (d // 8) % 4, (d // 2) % 4, d % 2
    s_next, s_prev = (s + 1) % 8, (s + 7) % 8
    d_next = (d + 1) % PEERS
    x_by = {1: (x + 1) % 4, -1: (x + 3) % 4, 2: (x + 2) % 4}
    y_by = {1: (y + 1) % 4, -1: (y + 3) % 4, 2: (y + 2) % 4}
    z = h * 8 + s
    z_next, z_prev = (z + 1) % 16, (z + 15) % 16
    near, far = z_prev // 8, 1 - z_prev // 8

    def at(hh, xx, yy, cc):
        return hh * 32 + xx * 8 + yy * 2 + cc

    def x_peer(by):
        return (s, at(h, x_by[by], y, c))

    def y_peer(by):
        return (s, at(h, x, y_by[by], c))

    ahead = (s_next, at(z_next // 8, x, y, c))
    across = (s_next, at(1 - z_next // 8, x, y, c))
    behind = (s_prev, at(near, x, y, c))
    behind_across = (s_prev, at(far, x, y, c))
    four_up = ((s + 4) % 8, at((z + 4) % 16 // 8, x, y, c))
    four_down = ((s + 4) % 8, at((z + 12) % 16 // 8, x, y, c))
    relayed = (z + 11) % 16 // 8
    partner = (s, at(1 - h, x, y, c))
    sibling = (s, at(h, x, y, 1 - c))

    loads = [
        pltpu.make_async_copy(src, dst, local.at[i])
        for i, (src, dst) in enumerate(
            (
                (w_in, g_in.at[h, x, y, c]),
                (w_out_hbm, w_out),
                (dest_hbm, dest),
                (seg_hbm, seg),
                (patches, rows_v),
            )
        )
    ]
    for load in loads:
        load.start()

    barrier = pltpu.get_barrier_semaphore()

    near_by = (behind, behind_across, four_down, partner, sibling)
    near_by += tuple(map(x_peer, (1, -1, 2))) + tuple(map(y_peer, (1, -1, 2)))
    for peer in near_by:
        pl.semaphore_signal(barrier, inc=1, device_id=peer, device_id_type=MESH)

    for load in loads[:4]:
        load.wait()
    wide = w_out[...].astype(F32)
    out_piece[:, :512] = jnp.concatenate(
        [wide[:, 512 * j : 512 * (j + 1)] for j in range(4)], axis=0
    ).astype(BF16)
    to = dest[...]
    to_dev, to_slot = to // ROWS, to % ROWS
    note = iota((16, ROWS), 0)
    out_piece[:, 512:] = jnp.where(
        note == 0, to_dev, jnp.where(note == 1, to_slot, jnp.where(note == 2, seg[...], 0))
    ).astype(F32).astype(BF16)

    match = (iota((PEERS, ROWS), 0) == to_dev).astype(F32)
    before = (iota((ROWS, ROWS), 0) < iota((ROWS, ROWS), 1)).astype(F32).astype(BF16)
    earlier = dot(match.astype(BF16), before)
    rank = jnp.sum(earlier * match, axis=0, keepdims=True).astype(jnp.int32)
    line = iota((8 * PEERS, ROWS), 0)
    chosen = (line // 8 == to_dev) & (line % SLOTS == rank)
    pick_low = (chosen & (line % 8 < SLOTS)).astype(F32).astype(BF16)
    pick_high = (chosen & (line % 8 >= SLOTS)).astype(F32).astype(BF16)

    pl.semaphore_wait(barrier, len(near_by))

    copies = []

    def send(src, dst, peer):
        i = len(copies)
        copy = pltpu.make_async_remote_copy(
            src_ref=src,
            dst_ref=dst,
            send_sem=ss.at[i],
            recv_sem=rs.at[i],
            device_id=peer,
            device_id_type=MESH,
        )
        copy.start()
        copies.append(copy)
        return copy

    def spread(ref, peer):
        return send(ref, ref, peer)

    in_far = spread(g_in.at[h, x, y, c], partner)
    mine = g_qkv.at[h, x, y, c]
    mine, mine_o = g_qkv.at[h, x, y, c], g_proj.at[h, x, y, c]
    low, high = pl.ds(0, 768), pl.ds(768, 768)
    left, right = pl.ds(0, 1024), pl.ds(1024, 1024)
    low_far = send(w_query.at[:, low], mine.at[:, low], across)
    high_near = send(w_query.at[:, pl.ds(768, 256)], mine.at[:, pl.ds(768, 256)], ahead)
    kv_near = send(w_keyval, mine.at[:, pl.ds(1024, 512)], ahead)
    out_far = send(out_piece, g_out.at[h, x, y, c], across)
    low_near = send(w_query.at[:, low], mine.at[:, low], ahead)
    left_far = send(w_proj.at[:, left], mine_o.at[:, left], across)
    o_near = send(w_proj, mine_o, ahead)
    out_near = send(out_piece, g_out.at[h, x, y, c], ahead)

    class Unit:
        def __init__(self, ref, hh):
            self.ref, self.hh = ref, hh
            self.width = ref.shape[-1]
            self.split = self.width > 640
            self.ways = (1, -1) if self.split else (1, -1, 2)
            self.core, self.c1 = [], {}

        def block(self, lane, first, second, part=None):
            low, count = (0, 256) if lane == 0 else (256, 384)
            if self.width != 640:
                half = self.width // 2
                low, count = lane * half, half
            if part is not None:
                low, count = low + part * (half // 2), half // 2
            xx, yy = (first, second) if lane == 0 else (second, first)
            return self.ref.at[self.hh, xx, yy, c, :, pl.ds(low, count)]

        def one(self, lanes=(0, 1)):
            for way in (1, -1, 2):
                for lane in lanes:
                    a, b = (x, y) if lane == 0 else (y, x)
                    peer = x_peer if lane == 0 else y_peer
                    self.c1[lane, way] = spread(self.block(lane, a, b), peer(way))

        def three(self):
            self.c3 = {}
            for lane in (0, 1):
                b = y if lane == 0 else x
                peer = y_peer if lane == 0 else x_peer
                for way in (1, -1, 2):
                    self.c1[lane, way].wait_recv()
                whole = self.block(lane, ALL, b)
                for way in self.ways:
                    self.c3[lane, way] = spread(whole, peer(way))
                if self.split:
                    self.core.append(spread(whole, sibling))

        def four(self):
            self.c4 = {}
            for way in (1, -1):
                for lane in (0, 1):
                    by = y_by if lane == 0 else x_by
                    peer = y_peer if lane == 0 else x_peer
                    self.c3[lane, way].wait_recv()
                    self.c4[lane, way] = spread(
                        self.block(lane, ALL, by[-way], (1 - way) // 2), peer(way)
                    )
                    self.core.append(spread(self.block(lane, ALL, by[-way]), sibling))

        def five(self):
            for copy in (self.c4 if self.split else self.c3).values():
                copy.wait_recv()
            if not self.split:
                self.core.append(spread(self.ref.at[self.hh, :, :, c], sibling))
                return
            for lane in (0, 1):
                by = y_by if lane == 0 else x_by
                self.core.append(spread(self.block(lane, ALL, by[2]), sibling))

        def six(self):
            for copy in self.core:
                copy.wait_recv()

    u_in, u_out = Unit(g_in, ALL), Unit(g_out, ALL)
    u_qkv_n, u_qkv_f = Unit(g_qkv, near), Unit(g_qkv, far)
    u_o_n, u_o_f = Unit(g_proj, near), Unit(g_proj, far)

    high_near.wait_recv()
    kv_near.wait_recv()
    high_up = send(g_qkv.at[near, x, y, c, :, high], held_qkv, four_up)
    low_near.wait_recv()
    u_qkv_n.one()
    in_far.wait_recv()
    u_in.one()
    o_near.wait_recv()
    right_up = send(g_proj.at[near, x, y, c, :, right], held_o, four_up)
    u_o_n.one()
    u_in.three()
    u_qkv_n.three()
    high_up.wait_recv()
    high_far = send(held_qkv, g_qkv.at[relayed, x, y, c, :, high], four_up)
    out_near.wait_recv()
    out_far.wait_recv()
    u_out.one()
    u_in.five()
    right_up.wait_recv()
    right_far = send(held_o, g_proj.at[relayed, x, y, c, :, right], four_up)
    u_o_n.three()
    u_out.three()

    loads[4].wait()
    u_in.six()
    pl.semaphore_signal(ready, inc=1, device_id=behind, device_id_type=MESH)
    first = jax.nn.gelu(dot(rows_v[...], g_in[...].reshape(2048, 256))).astype(BF16)
    picked = dot(pick_low, first[:, :128]) + dot(pick_high, first[:, 128:])
    sent[...] = picked.reshape(PEERS, 8, 128).astype(BF16)

    def exchange(plane):
        def to_one(k, carry):
            e = plane * 32 + (d + k) % 32
            pltpu.make_async_remote_copy(
                src_ref=sent.at[e],
                dst_ref=got.at[d],
                send_sem=a2a_ss,
                recv_sem=a2a_rs,
                device_id=(s_next, e),
                device_id_type=MESH,
            ).start()
            return carry

        lax.fori_loop(0, 32, to_one, 0)

    pl.semaphore_wait(ready, 1)
    exchange(1 - z_next // 8)
    exchange(z_next // 8)

    low_far.wait_recv()
    u_qkv_f.one((0,))
    u_qkv_n.four()
    high_far.wait_recv()
    u_qkv_f.one((1,))
    u_o_n.four()
    left_far.wait_recv()
    u_o_f.one((0,))
    u_out.five()
    u_qkv_f.three()
    right_far.wait_recv()
    u_o_f.one((1,))
    u_qkv_n.five()
    u_o_n.five()
    u_o_f.three()

    u_out.six()
    wanted = iota((144, 1024), 0)
    line = iota((144, 1024), 1)
    owner = jnp.where(wanted < 128, wanted % PEERS, jnp.where(wanted == 128, d, (d + 63) % PEERS))
    kind = jnp.where(wanted < 64, 0, jnp.where(wanted < 128, 1, 2))
    notes = dot(
        (line == 16 * owner + kind).astype(F32).astype(BF16),
        g_out[:, :, :, :, :, pl.ds(512, 128)].reshape(1024, 128),
    )
    own, seg_before = notes[128:129], notes[129:130]
    here = (notes[:64] == d.astype(F32)).astype(F32)
    earlier = dot(here.astype(BF16), before)
    spot = here * (notes[64:128] + 1.0)
    line = iota((PEERS, 8 * PEERS), 1)
    valued = jnp.zeros((PEERS, 8 * PEERS), F32)
    for k in range(SLOTS):
        value = jnp.sum(jnp.where(earlier == float(k), spot, 0.0), axis=1, keepdims=True)
        valued = jnp.where(line % SLOTS == k, value, valued)
    valued = jnp.where(line // 8 == iota((PEERS, 8 * PEERS), 0), valued, 0.0)
    valued = jnp.sum(valued, axis=0, keepdims=True)
    put = iota((ROWS, 8 * PEERS), 0).astype(F32) + 1.0 == valued
    column = iota((ROWS, 8 * PEERS), 1)
    put_low = (put & (column % 8 < SLOTS)).astype(F32).astype(BF16)
    put_high = (put & (column % 8 >= SLOTS)).astype(F32).astype(BF16)

    u_qkv_f.four()
    pltpu.make_async_copy(got, got, a2a_rs).wait()
    arrived = got[...].astype(F32).reshape(8 * PEERS, 128).astype(BF16)
    packed[:, :128] = dot(put_low, arrived).astype(BF16)
    packed[:, 128:] = dot(put_high, arrived).astype(BF16)
    tail_copy = send(packed.at[pl.ds(ROWS - TAIL, TAIL)], tail, (s, d_next))
    u_o_f.four()

    spreader = (
        iota((256, 1024), 0) == 4 * (iota((256, 1024), 1) // 16) + iota((256, 1024), 1) % 4
    )
    spreader = spreader.astype(F32).astype(BF16)

    def embed(rows, start, count):
        wide = dot(rows, spreader)
        group = (iota((count, 1024), 1) % 16) // 4
        for j in range(4):
            lhs = jnp.where(group == j, wide, 0.0).astype(BF16)
            weights = g_out[:, :, :, :, :, pl.ds(0, 512)].reshape(1024, 512)
            emb[pl.ds(start, count), pl.ds(512 * j, 512)] = dot(lhs, weights).astype(BF16)
        residual = emb[pl.ds(start, count)].astype(F32)
        scale = lax.rsqrt(jnp.mean(residual * residual, axis=-1, keepdims=True) + 1e-05)
        normed[pl.ds(start, count)] = (residual * scale).astype(BF16)

    embed(packed[...], 0, ROWS)
    u_qkv_f.five()
    tail_copy.wait_recv()
    embed(tail[...], ROWS, TAIL)
    u_qkv_n.six()
    u_qkv_f.six()

    def project(j, carry):
        cols = pl.ds(pl.multiple_of(j * 256, 256), 256)
        weights = g_qkv[:, :, :, :, :, cols].reshape(2048, 256)
        qkv[:, cols] = dot(normed[...], weights).astype(BF16)
        return carry

    lax.fori_loop(0, 6, project, 0)
    u_o_f.five()

    square = iota((ROWS, ROWS), 0) == iota((ROWS, ROWS), 1)
    row_seg = jnp.sum(jnp.where(square, own, 0.0), axis=1, keepdims=True)
    key_seg = jnp.concatenate([own, pltpu.roll(seg_before, TAIL, 1)], axis=1)[:, : ROWS + TAIL]
    key = iota((ROWS, ROWS + TAIL), 1)
    row = iota((ROWS, ROWS + TAIL), 0)
    allowed = (key_seg == row_seg) & ((key <= row) | ((key >= ROWS) & (d > 0)))
    low = iota((ROWS + TAIL, 128), 1) < HEAD_WIDTH
    zero = jnp.zeros((ROWS + TAIL, 128), F32)

    def sides(tile, group):
        tile = tile.astype(F32)
        turned = pltpu.roll(tile, HEAD_WIDTH, 1)
        here, there = (tile, turned) if group == 0 else (turned, tile)
        return (
            jnp.where(low, here, zero).astype(BF16),
            jnp.where(low, zero, there).astype(BF16),
        )

    for pair in range(2):
        keys_tile = qkv[:, pl.ds(1024 + 128 * pair, 128)]
        values_tile = qkv[:, pl.ds(1280 + 128 * pair, 128)]
        for group in range(2):
            keys = sides(keys_tile, group)
            values = sides(values_tile, group)
            for tile in range(2):
                cols = 256 * (2 * pair + group) + 128 * tile
                queries = qkv[:ROWS, pl.ds(cols, 128)]
                total = None
                for side in range(2):
                    scores = dot_nt(queries, keys[side]) * (1.0 / math.sqrt(HEAD_WIDTH))
                    scores = jnp.where(allowed, scores, -jnp.inf)
                    expon = jnp.exp(scores - jnp.max(scores, axis=-1, keepdims=True))
                    probs = (expon / jnp.sum(expon, axis=-1, keepdims=True)).astype(BF16)
                    part = dot(probs, values[side])
                    total = part if total is None else total + part
                ctx[:, pl.ds(cols, 128)] = total.astype(BF16)

    u_o_n.six()
    u_o_f.six()

    def finish(j, carry):
        cols = pl.ds(pl.multiple_of(j * 256, 256), 256)
        weights = g_proj[:, :, :, :, :, cols].reshape(1024, 256)
        added = dot(ctx[...], weights) + emb[pl.ds(0, ROWS), cols].astype(F32)
        out[:, cols] = added.astype(BF16)
        return carry

    lax.fori_loop(0, 8, finish, 0)

    for copy in copies:
        copy.wait_send()
    pltpu.make_async_copy(sent, sent, a2a_ss).wait()


def on_device(patches, pack_dest, seg_ids, w_patch_in, w_patch_out, w_query, w_keyval, w_attn_out):
    vmem = pl.BlockSpec(memory_space=pltpu.VMEM)
    hbm = pl.BlockSpec(memory_space=pltpu.HBM)
    grid = (2, 4, 4, 2)
    out = pl.pallas_call(
        kernel,
        out_shape=jax.ShapeDtypeStruct((ROWS, 2048), BF16),
        in_specs=[hbm] * 8,
        out_specs=vmem,
        scratch_shapes=[
            pltpu.VMEM((1, ROWS), jnp.int32),
            pltpu.VMEM((1, ROWS), jnp.int32),
            pltpu.VMEM((4, 2048), BF16),
            pltpu.VMEM((ROWS, 2048), BF16),
            pltpu.VMEM(grid + (32, 256), BF16),
            pltpu.VMEM(grid + (16, 640), BF16),
            pltpu.VMEM(grid + (32, 1536), BF16),
            pltpu.VMEM(grid + (16, 2048), BF16),
            pltpu.VMEM((16, 640), BF16),
            pltpu.VMEM((32, 768), BF16),
            pltpu.VMEM((16, 1024), BF16),
            pltpu.VMEM((PEERS, 8, 128), BF16),
            pltpu.VMEM((PEERS, 8, 128), BF16),
            pltpu.VMEM((ROWS, 256), BF16),
            pltpu.VMEM((TAIL, 256), BF16),
            pltpu.VMEM((ROWS + TAIL, 2048), BF16),
            pltpu.VMEM((ROWS + TAIL, 2048), BF16),
            pltpu.VMEM((ROWS + TAIL, 1536), BF16),
            pltpu.VMEM((ROWS, 1024), BF16),
            pltpu.SemaphoreType.DMA((180,)),
            pltpu.SemaphoreType.DMA((180,)),
            pltpu.SemaphoreType.DMA,
            pltpu.SemaphoreType.DMA,
            pltpu.SemaphoreType.DMA((5,)),
            pltpu.SemaphoreType.REGULAR,
        ],
        compiler_params=pltpu.CompilerParams(
            collective_id=0, has_side_effects=True, vmem_limit_bytes=64 << 20
        ),
        name="layer",
    )(
        patches[0],
        pack_dest,
        seg_ids,
        w_patch_in[0],
        w_patch_out[0],
        w_query[0],
        w_keyval[0],
        w_attn_out[0],
    )
    return out[None]


def solution(mesh):
    in_specs = (
        P("section", "dp", None),
        P("section", "dp"),
        P("section", "dp"),
        P("section", "dp", None),
        P("section", "dp", None),
        P("section", "dp", None),
        P("section", "dp", None),
        P("section", "dp", None),
    )
    out_specs = P("section", "dp", None)
    return jax.shard_map(
        on_device, mesh=mesh, in_specs=in_specs, out_specs=out_specs, check_vma=False
    )
```

```python
import math

import jax
import jax.numpy as jnp
from jax import lax
from jax.experimental import pallas as pl
from jax.experimental.pallas import tpu as pltpu
from jax.sharding import PartitionSpec as P

HEADS = 16
KV_HEADS = 4
HEAD_WIDTH = 64
ROWS = 128
TAIL = 32
SLOTS = 4
PEERS = 64
MESH = pl.DeviceIdType.MESH
F32 = jnp.float32
BF16 = jnp.bfloat16
ALL = slice(None)


def iota(shape, dim):
    return lax.broadcasted_iota(jnp.int32, shape, dim)


def dot(a, b):
    return jnp.dot(a, b, preferred_element_type=F32)


def dot_nt(a, b):
    return lax.dot_general(a, b, (((1,), (1,)), ((), ())), preferred_element_type=F32)


def kernel(
    patches,
    dest_hbm,
    seg_hbm,
    w_in,
    w_out_hbm,
    w_query,
    w_keyval,
    w_proj,
    out,
    dest,
    seg,
    w_out,
    rows_v,
    g_in,
    g_out,
    g_qkv,
    g_proj,
    out_piece,
    held_qkv,
    held_o,
    sent,
    got,
    packed,
    tail,
    emb,
    normed,
    qkv,
    ctx,
    partial,
    ss,
    rs,
    a2a_ss,
    a2a_rs,
    local,
    ready,
):
    s = lax.axis_index("section")
    d = lax.axis_index("dp")
    h, x, y, c = d // 32, (d // 8) % 4, (d // 2) % 4, d % 2
    s_next, s_prev = (s + 1) % 8, (s + 7) % 8
    d_next = (d + 1) % PEERS
    x_by = {1: (x + 1) % 4, -1: (x + 3) % 4, 2: (x + 2) % 4}
    y_by = {1: (y + 1) % 4, -1: (y + 3) % 4, 2: (y + 2) % 4}
    z = h * 8 + s
    z_next, z_prev = (z + 1) % 16, (z + 15) % 16
    near, far = z_prev // 8, 1 - z_prev // 8

    def at(hh, xx, yy, cc):
        return hh * 32 + xx * 8 + yy * 2 + cc

    def x_peer(by):
        return (s, at(h, x_by[by], y, c))

    def y_peer(by):
        return (s, at(h, x, y_by[by], c))

    ahead = (s_next, at(z_next // 8, x, y, c))
    across = (s_next, at(1 - z_next // 8, x, y, c))
    behind = (s_prev, at(near, x, y, c))
    behind_across = (s_prev, at(far, x, y, c))
    four_up = ((s + 4) % 8, at((z + 4) % 16 // 8, x, y, c))
    four_down = ((s + 4) % 8, at((z + 12) % 16 // 8, x, y, c))
    relayed = (z + 11) % 16 // 8
    partner = (s, at(1 - h, x, y, c))
    sibling = (s, at(h, x, y, 1 - c))

    loads = [
        pltpu.make_async_copy(src, dst, local.at[i])
        for i, (src, dst) in enumerate(
            (
                (w_in, g_in.at[h, x, y, c]),
                (w_out_hbm, w_out),
                (dest_hbm, dest),
                (seg_hbm, seg),
                (patches, rows_v),
            )
        )
    ]
    for load in loads:
        load.start()

    barrier = pltpu.get_barrier_semaphore()

    near_by = (behind, behind_across, four_down, partner, sibling)
    near_by += tuple(map(x_peer, (1, -1, 2))) + tuple(map(y_peer, (1, -1, 2)))
    for peer in near_by:
        pl.semaphore_signal(barrier, inc=1, device_id=peer, device_id_type=MESH)

    for load in loads[:4]:
        load.wait()
    wide = w_out[...].astype(F32)
    out_piece[:, :512] = jnp.concatenate(
        [wide[:, 512 * j : 512 * (j + 1)] for j in range(4)], axis=0
    ).astype(BF16)
    to = dest[...]
    to_dev, to_slot = to // ROWS, to % ROWS
    note = iota((16, ROWS), 0)
    out_piece[:, 512:] = jnp.where(
        note == 0, to_dev, jnp.where(note == 1, to_slot, jnp.where(note == 2, seg[...], 0))
    ).astype(F32).astype(BF16)

    match = (iota((PEERS, ROWS), 0) == to_dev).astype(F32)
    before = (iota((ROWS, ROWS), 0) < iota((ROWS, ROWS), 1)).astype(F32).astype(BF16)
    earlier = dot(match.astype(BF16), before)
    rank = jnp.sum(earlier * match, axis=0, keepdims=True).astype(jnp.int32)
    line = iota((8 * PEERS, ROWS), 0)
    chosen = (line // 8 == to_dev) & (line % SLOTS == rank)
    pick_low = (chosen & (line % 8 < SLOTS)).astype(F32).astype(BF16)
    pick_high = (chosen & (line % 8 >= SLOTS)).astype(F32).astype(BF16)

    pl.semaphore_wait(barrier, len(near_by))

    copies = []

    def send(src, dst, peer):
        i = len(copies)
        copy = pltpu.make_async_remote_copy(
            src_ref=src,
            dst_ref=dst,
            send_sem=ss.at[i],
            recv_sem=rs.at[i],
            device_id=peer,
            device_id_type=MESH,
        )
        copy.start()
        copies.append(copy)
        return copy

    def spread(ref, peer):
        return send(ref, ref, peer)

    in_far = spread(g_in.at[h, x, y, c], partner)
    mine = g_qkv.at[h, x, y, c]
    mine, mine_o = g_qkv.at[h, x, y, c], g_proj.at[h, x, y, c]
    low, high = pl.ds(0, 768), pl.ds(768, 768)
    left, right = pl.ds(0, 1024), pl.ds(1024, 1024)
    low_far = send(w_query.at[:, low], mine.at[:, low], across)
    high_near = send(w_query.at[:, pl.ds(768, 256)], mine.at[:, pl.ds(768, 256)], ahead)
    kv_near = send(w_keyval, mine.at[:, pl.ds(1024, 512)], ahead)
    out_far = send(out_piece, g_out.at[h, x, y, c], across)
    low_near = send(w_query.at[:, low], mine.at[:, low], ahead)
    left_far = send(w_proj.at[:, left], mine_o.at[:, left], across)
    o_near = send(w_proj, mine_o, ahead)
    out_near = send(out_piece, g_out.at[h, x, y, c], ahead)

    class Unit:
        def __init__(self, ref, hh):
            self.ref, self.hh = ref, hh
            self.width = ref.shape[-1]
            self.split = self.width > 640
            self.ways = (1, -1) if self.split else (2, 1, -1)
            self.core, self.c1 = [], {}

        def block(self, lane, first, second, part=None):
            low, count = (0, 256) if lane == 0 else (256, 384)
            if self.width != 640:
                half = self.width // 2
                low, count = lane * half, half
            if part is not None:
                low, count = low + part * (half // 2), half // 2
            xx, yy = (first, second) if lane == 0 else (second, first)
            return self.ref.at[self.hh, xx, yy, c, :, pl.ds(low, count)]

        def one(self, lanes=(0, 1)):
            for way in (2, 1, -1):
                for lane in lanes:
                    a, b = (x, y) if lane == 0 else (y, x)
                    peer = x_peer if lane == 0 else y_peer
                    self.c1[lane, way] = spread(self.block(lane, a, b), peer(way))

        def three(self):
            self.c3 = {}
            for lane in (0, 1):
                b = y if lane == 0 else x
                peer = y_peer if lane == 0 else x_peer
                for way in (1, -1, 2):
                    self.c1[lane, way].wait_recv()
                whole = self.block(lane, ALL, b)
                for way in self.ways:
                    self.c3[lane, way] = spread(whole, peer(way))
                if self.split:
                    self.core.append(spread(whole, sibling))

        def four(self):
            self.c4 = {}
            for way in (1, -1):
                for lane in (0, 1):
                    by = y_by if lane == 0 else x_by
                    peer = y_peer if lane == 0 else x_peer
                    self.c3[lane, way].wait_recv()
                    self.c4[lane, way] = spread(
                        self.block(lane, ALL, by[-way], (1 - way) // 2), peer(way)
                    )
                    self.core.append(spread(self.block(lane, ALL, by[-way]), sibling))

        def five(self):
            for copy in (self.c4 if self.split else self.c3).values():
                copy.wait_recv()
            if not self.split:
                self.core.append(spread(self.ref.at[self.hh, :, :, c], sibling))
                return
            for lane in (0, 1):
                by = y_by if lane == 0 else x_by
                self.core.append(spread(self.block(lane, ALL, by[2]), sibling))

        def six(self):
            for copy in self.core:
                copy.wait_recv()

    u_in, u_out = Unit(g_in, ALL), Unit(g_out, ALL)
    u_qkv_n, u_qkv_f = Unit(g_qkv, near), Unit(g_qkv, far)
    u_o_n, u_o_f = Unit(g_proj, near), Unit(g_proj, far)

    high_near.wait_recv()
    kv_near.wait_recv()
    high_up = send(g_qkv.at[near, x, y, c, :, high], held_qkv, four_up)
    low_near.wait_recv()
    u_qkv_n.one()
    in_far.wait_recv()
    u_in.one()
    o_near.wait_recv()
    right_up = send(g_proj.at[near, x, y, c, :, right], held_o, four_up)
    u_o_n.one()
    u_in.three()
    u_qkv_n.three()
    high_up.wait_recv()
    high_far = send(held_qkv, g_qkv.at[relayed, x, y, c, :, high], four_up)
    out_near.wait_recv()
    out_far.wait_recv()
    u_out.one()
    u_in.five()
    right_up.wait_recv()
    right_far = send(held_o, g_proj.at[relayed, x, y, c, :, right], four_up)
    u_o_n.three()
    u_out.three()

    loads[4].wait()
    u_in.six()
    pl.semaphore_signal(ready, inc=1, device_id=behind, device_id_type=MESH)
    first = jax.nn.gelu(dot(rows_v[...], g_in[...].reshape(2048, 256))).astype(BF16)
    picked = dot(pick_low, first[:, :128]) + dot(pick_high, first[:, 128:])
    sent[...] = picked.reshape(PEERS, 8, 128).astype(BF16)

    def exchange(plane):
        def to_one(k, carry):
            e = plane * 32 + (d + k) % 32
            pltpu.make_async_remote_copy(
                src_ref=sent.at[e],
                dst_ref=got.at[d],
                send_sem=a2a_ss,
                recv_sem=a2a_rs,
                device_id=(s_next, e),
                device_id_type=MESH,
            ).start()
            return carry

        lax.fori_loop(0, 32, to_one, 0)

    pl.semaphore_wait(ready, 1)
    exchange(1 - z_next // 8)
    exchange(z_next // 8)

    low_far.wait_recv()
    u_qkv_f.one((0,))
    u_qkv_n.four()
    high_far.wait_recv()
    u_qkv_f.one((1,))
    u_o_n.four()
    left_far.wait_recv()
    u_o_f.one((0,))
    u_out.five()
    u_qkv_f.three()
    right_far.wait_recv()
    u_o_f.one((1,))
    u_qkv_n.five()
    u_o_n.five()
    u_o_f.three()

    u_out.six()
    wanted = iota((144, 1024), 0)
    line = iota((144, 1024), 1)
    owner = jnp.where(wanted < 128, wanted % PEERS, jnp.where(wanted == 128, d, (d + 63) % PEERS))
    kind = jnp.where(wanted < 64, 0, jnp.where(wanted < 128, 1, 2))
    notes = dot(
        (line == 16 * owner + kind).astype(F32).astype(BF16),
        g_out[:, :, :, :, :, pl.ds(512, 128)].reshape(1024, 128),
    )
    own, seg_before = notes[128:129], notes[129:130]
    here = (notes[:64] == d.astype(F32)).astype(F32)
    earlier = dot(here.astype(BF16), before)
    spot = here * (notes[64:128] + 1.0)
    line = iota((PEERS, 8 * PEERS), 1)
    valued = jnp.zeros((PEERS, 8 * PEERS), F32)
    for k in range(SLOTS):
        value = jnp.sum(jnp.where(earlier == float(k), spot, 0.0), axis=1, keepdims=True)
        valued = jnp.where(line % SLOTS == k, value, valued)
    valued = jnp.where(line // 8 == iota((PEERS, 8 * PEERS), 0), valued, 0.0)
    valued = jnp.sum(valued, axis=0, keepdims=True)
    put = iota((ROWS, 8 * PEERS), 0).astype(F32) + 1.0 == valued
    column = iota((ROWS, 8 * PEERS), 1)
    put_low = (put & (column % 8 < SLOTS)).astype(F32).astype(BF16)
    put_high = (put & (column % 8 >= SLOTS)).astype(F32).astype(BF16)

    u_qkv_f.four()
    pltpu.make_async_copy(got, got, a2a_rs).wait()
    arrived = got[...].astype(F32).reshape(8 * PEERS, 128).astype(BF16)
    packed[:, :128] = dot(put_low, arrived).astype(BF16)
    packed[:, 128:] = dot(put_high, arrived).astype(BF16)
    tail_copy = send(packed.at[pl.ds(ROWS - TAIL, TAIL)], tail, (s, d_next))
    u_o_f.four()

    spreader = (
        iota((256, 1024), 0) == 4 * (iota((256, 1024), 1) // 16) + iota((256, 1024), 1) % 4
    )
    spreader = spreader.astype(F32).astype(BF16)

    def embed(rows, start, count):
        wide = dot(rows, spreader)
        group = (iota((count, 1024), 1) % 16) // 4
        for j in range(4):
            lhs = jnp.where(group == j, wide, 0.0).astype(BF16)
            weights = g_out[:, :, :, :, :, pl.ds(0, 512)].reshape(1024, 512)
            emb[pl.ds(start, count), pl.ds(512 * j, 512)] = dot(lhs, weights).astype(BF16)
        residual = emb[pl.ds(start, count)].astype(F32)
        scale = lax.rsqrt(jnp.mean(residual * residual, axis=-1, keepdims=True) + 1e-05)
        normed[pl.ds(start, count)] = (residual * scale).astype(BF16)

    embed(packed[...], 0, ROWS)
    u_qkv_f.five()
    tail_copy.wait_recv()
    embed(tail[...], ROWS, TAIL)
    u_qkv_n.six()
    u_qkv_f.six()

    def project(j, carry):
        cols = pl.ds(pl.multiple_of(j * 256, 256), 256)
        weights = g_qkv[:, :, :, :, :, cols].reshape(2048, 256)
        qkv[:, cols] = dot(normed[...], weights).astype(BF16)
        return carry

    lax.fori_loop(0, 6, project, 0)
    u_o_f.five()

    square = iota((ROWS, ROWS), 0) == iota((ROWS, ROWS), 1)
    row_seg = jnp.sum(jnp.where(square, own, 0.0), axis=1, keepdims=True)
    key_seg = jnp.concatenate([own, pltpu.roll(seg_before, TAIL, 1)], axis=1)[:, : ROWS + TAIL]
    key = iota((ROWS, ROWS + TAIL), 1)
    row = iota((ROWS, ROWS + TAIL), 0)
    allowed = (key_seg == row_seg) & ((key <= row) | ((key >= ROWS) & (d > 0)))
    low = iota((ROWS + TAIL, 128), 1) < HEAD_WIDTH
    zero = jnp.zeros((ROWS + TAIL, 128), F32)

    def sides(tile, group):
        tile = tile.astype(F32)
        turned = pltpu.roll(tile, HEAD_WIDTH, 1)
        here, there = (tile, turned) if group == 0 else (turned, tile)
        return (
            jnp.where(low, here, zero).astype(BF16),
            jnp.where(low, zero, there).astype(BF16),
        )

    for pair in range(2):
        keys_tile = qkv[:, pl.ds(1024 + 128 * pair, 128)]
        values_tile = qkv[:, pl.ds(1280 + 128 * pair, 128)]
        for group in range(2):
            keys = sides(keys_tile, group)
            values = sides(values_tile, group)
            for tile in range(2):
                cols = 256 * (2 * pair + group) + 128 * tile
                queries = qkv[:ROWS, pl.ds(cols, 128)]
                total = None
                for side in range(2):
                    scores = dot_nt(queries, keys[side]) * (1.0 / math.sqrt(HEAD_WIDTH))
                    scores = jnp.where(allowed, scores, -jnp.inf)
                    expon = jnp.exp(scores - jnp.max(scores, axis=-1, keepdims=True))
                    probs = (expon / jnp.sum(expon, axis=-1, keepdims=True)).astype(BF16)
                    part = dot(probs, values[side])
                    total = part if total is None else total + part
                ctx[:, pl.ds(cols, 128)] = total.astype(BF16)

    def half(hh, cols):
        context = ctx[:, pl.ds(pl.multiple_of(hh * 512, 512), 512)]
        return dot(context, g_proj[hh, :, :, :, :, cols].reshape(512, 512))

    def begin(j, carry):
        cols = pl.ds(pl.multiple_of(j * 512, 512), 512)
        partial[:, cols] = half(near, cols) + emb[pl.ds(0, ROWS), cols].astype(F32)
        return carry

    def finish(j, carry):
        cols = pl.ds(pl.multiple_of(j * 512, 512), 512)
        out[:, cols] = (partial[:, cols] + half(far, cols)).astype(BF16)
        return carry

    u_o_n.six()
    lax.fori_loop(0, 4, begin, 0)
    u_o_f.six()
    lax.fori_loop(0, 4, finish, 0)

    for copy in copies:
        copy.wait_send()
    pltpu.make_async_copy(sent, sent, a2a_ss).wait()


def on_device(patches, pack_dest, seg_ids, w_patch_in, w_patch_out, w_query, w_keyval, w_attn_out):
    vmem = pl.BlockSpec(memory_space=pltpu.VMEM)
    hbm = pl.BlockSpec(memory_space=pltpu.HBM)
    grid = (2, 4, 4, 2)
    out = pl.pallas_call(
        kernel,
        out_shape=jax.ShapeDtypeStruct((ROWS, 2048), BF16),
        in_specs=[hbm] * 8,
        out_specs=vmem,
        scratch_shapes=[
            pltpu.VMEM((1, ROWS), jnp.int32),
            pltpu.VMEM((1, ROWS), jnp.int32),
            pltpu.VMEM((4, 2048), BF16),
            pltpu.VMEM((ROWS, 2048), BF16),
            pltpu.VMEM(grid + (32, 256), BF16),
            pltpu.VMEM(grid + (16, 640), BF16),
            pltpu.VMEM(grid + (32, 1536), BF16),
            pltpu.VMEM(grid + (16, 2048), BF16),
            pltpu.VMEM((16, 640), BF16),
            pltpu.VMEM((32, 768), BF16),
            pltpu.VMEM((16, 1024), BF16),
            pltpu.VMEM((PEERS, 8, 128), BF16),
            pltpu.VMEM((PEERS, 8, 128), BF16),
            pltpu.VMEM((ROWS, 256), BF16),
            pltpu.VMEM((TAIL, 256), BF16),
            pltpu.VMEM((ROWS + TAIL, 2048), BF16),
            pltpu.VMEM((ROWS + TAIL, 2048), BF16),
            pltpu.VMEM((ROWS + TAIL, 1536), BF16),
            pltpu.VMEM((ROWS, 1024), BF16),
            pltpu.VMEM((ROWS, 2048), F32),
            pltpu.SemaphoreType.DMA((180,)),
            pltpu.SemaphoreType.DMA((180,)),
            pltpu.SemaphoreType.DMA,
            pltpu.SemaphoreType.DMA,
            pltpu.SemaphoreType.DMA((5,)),
            pltpu.SemaphoreType.REGULAR,
        ],
        compiler_params=pltpu.CompilerParams(
            collective_id=0, has_side_effects=True, vmem_limit_bytes=64 << 20
        ),
        name="layer",
    )(
        patches[0],
        pack_dest,
        seg_ids,
        w_patch_in[0],
        w_patch_out[0],
        w_query[0],
        w_keyval[0],
        w_attn_out[0],
    )
    return out[None]


def solution(mesh):
    in_specs = (
        P("section", "dp", None),
        P("section", "dp"),
        P("section", "dp"),
        P("section", "dp", None),
        P("section", "dp", None),
        P("section", "dp", None),
        P("section", "dp", None),
        P("section", "dp", None),
    )
    out_specs = P("section", "dp", None)
    return jax.shard_map(
        on_device, mesh=mesh, in_specs=in_specs, out_specs=out_specs, check_vma=False
    )
```
